32 devices in a mesh: owner: 4 (over z), lane: 8 (over y, x, core).
Axes of the slice: x: 2, y: 2, z: 4, core: 2. Of those that a mesh axis runs over, the one named last changes fastest.
Arguments:
- tokens: bfloat16 [16384, 4096], P(('owner', 'lane')), may hold values from -6 to 6
- value_base_weight: bfloat16 [4096, 1024], P('lane'), may hold values from -0.09375 to 0.09375
- adapter_down: bfloat16 [4096, 32768], P(None, ('owner', 'lane')), may hold values from -0.09375 to 0.09375
- adapter_up: bfloat16 [32768, 1024], P(('owner', 'lane')), may hold values from -0.75 to 0.75
- adapter_per_row: int32 [16384], P(('owner', 'lane')), may hold values from 0 to 511, as said below
- frequent_adapter: int32 [8], replicated, may hold values from 0 to 511, as said below
Outputs:
- values_out: bfloat16 [16384, 1024], P(('owner', 'lane'))
The draws below stay inside these ranges and needn't reach their ends.
Inputs may be any that keep to these rules, and one draw needn't show every extreme that they name: `adapter_per_row`: adapter a belongs to device a // 16 of owner+lane in mesh order. Of the rows of one device, exactly 96 have an adapter not in frequent_adapter, and at most 4 of these belong to any one device; in every draw one device receives exactly 4 such rows from every device. The other rows have hot adapters. `frequent_adapter`: 8 distinct adapters, belonging to distinct devices; adapter 512 - 1 is always one of them.
All inputs are finite; a program needn't handle non-finite values.
Results may differ from the reference program's by a relative error of at most 0.0055.
Values may be sent and summed in bfloat16 or wider, within the bound.
A program may use at most 192 MiB of HBM per device.

```python
import jax
import jax.numpy as jnp
from jax import lax

MODEL_WIDTH = 4096
VALUE_WIDTH = 1024
ADAPTER_RANK = 64
ADAPTERS_DEVICE = 16
HOT = 8
CAP = 4
ROW_DEV = 512
ADAPTER_TOTAL = 512
ROWS = 16384
COLD_DEV = 96
N_OWNER = 4
N_LANE = 8


def common_draw(key):
    devices = N_OWNER * N_LANE
    subkeys = jax.random.split(jax.random.fold_in(key, 7), 9)
    center = jax.random.randint(subkeys[0], (), 0, devices - 1)
    ordering = jax.random.permutation(subkeys[1], devices - 2)
    others = (center + 1 + ordering[:HOT - 1]) % (devices - 1)
    hot_device = jnp.concatenate([jnp.full((1,), devices - 1, jnp.int32), others.astype(jnp.int32)])
    other_slot = jax.random.randint(subkeys[2], (HOT - 1,), 0, ADAPTERS_DEVICE)
    hot_slot = jnp.concatenate([jnp.full((1,), ADAPTERS_DEVICE - 1, jnp.int32), other_slot.astype(jnp.int32)])
    order_hot = jax.random.permutation(subkeys[8], HOT)
    hot_device = hot_device[order_hot]
    hot_slot = hot_slot[order_hot]
    hot_list = (hot_device * ADAPTERS_DEVICE + hot_slot).astype(jnp.int32)
    held_slot = jnp.full((devices,), -1, jnp.int32).at[hot_device].set(hot_slot)
    pool_dest = (center + 1 + jnp.arange((devices - 1) * CAP) // CAP) % devices
    shuffled = jax.vmap(lambda subkey: jax.random.permutation(subkey, pool_dest))(jax.random.split(subkeys[3], devices))
    extra_dest = shuffled[:, :COLD_DEV - CAP]
    destinations = jnp.concatenate([jnp.full((devices, CAP), center, jnp.int32), extra_dest.astype(jnp.int32)], axis=1)
    shift_draw = jax.random.randint(subkeys[4], (devices, COLD_DEV), 0, ADAPTERS_DEVICE - 1)
    free_draw = jax.random.randint(subkeys[5], (devices, COLD_DEV), 0, ADAPTERS_DEVICE)
    owned_slot = held_slot[destinations]
    slots = jnp.where(owned_slot >= 0, (owned_slot + 1 + shift_draw) % ADAPTERS_DEVICE, free_draw)
    cold_rows = destinations * ADAPTERS_DEVICE + slots
    hot_pick = jax.random.randint(subkeys[6], (devices, ROW_DEV - COLD_DEV), 0, HOT)
    hot_rows = hot_list[hot_pick]
    all_rows = jnp.concatenate([cold_rows, hot_rows], axis=1).astype(jnp.int32)
    shuffled_rows = jax.vmap(lambda subkey, line: jax.random.permutation(subkey, line))(jax.random.split(subkeys[7], devices), all_rows)
    return (hot_list, shuffled_rows.reshape(-1).astype(jnp.int32))


def draw_adapter_per_row(key, part):
    return common_draw(key)[1]


def draw_frequent_adapter(key, part):
    return common_draw(key)[0]


def block_scale(stream_key, dims, shards, least, top_value):
    level = 1.0
    for position, parts in shards:
        heights = jax.random.uniform(jax.random.fold_in(jax.random.fold_in(stream_key, 6), position), (parts,), jnp.float32, least / len(shards), top_value / len(shards))
        level = level * jnp.repeat(jnp.exp(heights), dims[position] // parts).reshape((-1,) + (1,) * (len(dims) - 1 - position))
    return level


def centred(own_key, extent, deviation, bound, cuts=(), kind=jnp.bfloat16):
    result = jax.random.normal(own_key, extent, jnp.float32) * deviation
    if len(cuts) > 0:
        result = block_scale(own_key, extent, cuts, -0.22, 0.18) * result
    return jnp.clip(result, min=-bound, max=bound).astype(kind)


def setup_inputs(seed: int = 0) -> dict:
    streams_of = jax.random.split(jax.random.key(seed), 7)
    tokens = centred(streams_of[0], (ROWS, MODEL_WIDTH), 1.0, 6.0, ((0, 32),))
    value_base_weight = centred(streams_of[1], (MODEL_WIDTH, VALUE_WIDTH), MODEL_WIDTH ** -0.5, 0.09375, ((0, 8),))
    adapter_down = centred(streams_of[2], (MODEL_WIDTH, ADAPTER_TOTAL * ADAPTER_RANK), MODEL_WIDTH ** -0.5, 0.09375, ((1, 32),))
    adapter_up = centred(streams_of[3], (ADAPTER_TOTAL * ADAPTER_RANK, VALUE_WIDTH), ADAPTER_RANK ** -0.5, 0.75, ((0, 32),))
    adapter_per_row = draw_adapter_per_row(jax.random.fold_in(streams_of[6], 71), 0)
    frequent_adapter = draw_frequent_adapter(jax.random.fold_in(streams_of[6], 71), 0)
    return {"tokens": tokens, "value_base_weight": value_base_weight, "adapter_down": adapter_down, "adapter_up": adapter_up, "adapter_per_row": adapter_per_row, "frequent_adapter": frequent_adapter}


ADAPTER_SCALE = 2.0


def reference(tokens, value_base_weight, adapter_down, adapter_up, adapter_per_row, frequent_adapter):
    devices = N_OWNER * N_LANE
    base_output = jnp.dot(tokens, value_base_weight, preferred_element_type=jnp.float32)
    down_tensor_three = adapter_down.reshape(MODEL_WIDTH, ADAPTER_TOTAL, ADAPTER_RANK)
    up_tensor_three = adapter_up.reshape(ADAPTER_TOTAL, ADAPTER_RANK, VALUE_WIDTH)
    hot_down = down_tensor_three[:, frequent_adapter, :].reshape(MODEL_WIDTH, HOT * ADAPTER_RANK)
    hot_up = up_tensor_three[frequent_adapter].reshape(HOT * ADAPTER_RANK, VALUE_WIDTH)
    match = adapter_per_row[:, None] == frequent_adapter[None, :]
    is_hot = jnp.any(match, axis=1)

    def hot_block(pieces):
        block_rows, block_match = pieces
        column_mask = jnp.repeat(block_match, ADAPTER_RANK, axis=1)
        rank_projection = jnp.where(column_mask, jnp.dot(block_rows, hot_down, preferred_element_type=jnp.float32), 0.0).astype(jnp.bfloat16)
        return jnp.dot(rank_projection, hot_up, preferred_element_type=jnp.float32).astype(jnp.bfloat16)

    hot_delta = lax.map(hot_block, (tokens.reshape(devices, ROW_DEV, MODEL_WIDTH), match.reshape(devices, ROW_DEV, HOT)))
    hot_delta = hot_delta.reshape(ROWS, VALUE_WIDTH)

    owner_dev = (adapter_per_row // ADAPTERS_DEVICE).astype(jnp.int32)
    sort_key = jnp.where(is_hot, devices, owner_dev).astype(jnp.int32)
    ordering = jnp.argsort(sort_key, stable=True).astype(jnp.int32)
    counts = jnp.sum((sort_key[:, None] == jnp.arange(devices, dtype=jnp.int32)[None, :]).astype(jnp.int32), axis=0)
    offsets = (jnp.cumsum(counts) - counts).astype(jnp.int32)
    span = devices * CAP
    padded = jnp.concatenate([ordering, jnp.full((span,), ROWS, jnp.int32)])

    def cold_block(device_index):
        index = lax.dynamic_slice_in_dim(padded, offsets[device_index], span).astype(jnp.int32)
        valid = jnp.arange(span, dtype=jnp.int32) < counts[device_index]
        safe_index = jnp.where(valid, index, 0).astype(jnp.int32)
        block_rows = tokens[safe_index]
        labels = jnp.where(valid, adapter_per_row[safe_index] % ADAPTERS_DEVICE, -1)
        down_matrix_block = lax.dynamic_slice_in_dim(adapter_down, (device_index * ADAPTERS_DEVICE * ADAPTER_RANK).astype(jnp.int32), ADAPTERS_DEVICE * ADAPTER_RANK, 1)
        up_matrix_block = lax.dynamic_slice_in_dim(adapter_up, (device_index * ADAPTERS_DEVICE * ADAPTER_RANK).astype(jnp.int32), ADAPTERS_DEVICE * ADAPTER_RANK, 0)
        column_holder = jnp.arange(ADAPTERS_DEVICE * ADAPTER_RANK, dtype=jnp.int32) // ADAPTER_RANK
        rank_projection = jnp.where(column_holder[None, :] == labels[:, None], jnp.dot(block_rows, down_matrix_block, preferred_element_type=jnp.float32), 0.0).astype(jnp.bfloat16)
        adapter_delta = jnp.dot(rank_projection, up_matrix_block, preferred_element_type=jnp.float32).astype(jnp.bfloat16)
        return jnp.where(valid, index, ROWS).astype(jnp.int32), adapter_delta

    indices, deltas = lax.map(cold_block, jnp.arange(devices, dtype=jnp.int32))
    cold_delta = jnp.zeros((ROWS, VALUE_WIDTH), jnp.bfloat16).at[indices.reshape(-1)].set(deltas.reshape(-1, VALUE_WIDTH), mode="drop")
    adapter_delta = jnp.where(is_hot[:, None], hot_delta, cold_delta)
    return (base_output + ADAPTER_SCALE * adapter_delta.astype(jnp.float32)).astype(jnp.bfloat16)
```

```python
import functools

import jax
import jax.numpy as jnp
from jax import lax
from jax.experimental import pallas as pl
from jax.experimental.pallas import tpu as pltpu
from jax.sharding import PartitionSpec as P

ADAPTER_RANK = 64
ADAPTERS_DEVICE = 16
HOT = 8
CAP = 4


ADAPTER_SCALE = 2.0

MESH = pl.DeviceIdType.MESH
ANY = pl.BlockSpec(memory_space=pl.ANY)


def remote(src, dst, send, recv, at):
    return pltpu.make_async_remote_copy(
        src_ref=src, dst_ref=dst, send_sem=send, recv_sem=recv, device_id=at, device_id_type=MESH
    )


def position_of(nl):
    o, l = lax.axis_index("owner"), lax.axis_index("lane")
    return o, l, o * nl + l, (o, l + 1 - 2 * lax.rem(l, 2))


def all_to_all(me, nl, n, pairs, send, recv):
    def copies(k):
        to = lax.rem(me + k, n)
        at = (lax.div(to, nl), lax.rem(to, nl))
        return [
            remote(src(to), dst, send.at[i * n + k], recv.at[i * n + k], at)
            for i, (src, dst) in enumerate(pairs)
        ]

    def start():
        @pl.loop(1, n)
        def _(k):
            for c in copies(k):
                c.start()

    def wait():
        @pl.loop(1, n)
        def _(k):
            for c in copies(k):
                c.wait()

    return start, wait


def exchange_kernel(
    no, nl, w, rows, ups, downs, w_all, got, got_up, got_down,
    a_send, a_recv, w_send, w_recv, f_send, f_recv, local,
):
    n, half = no * nl, nl // 2
    o, l, me, partner = position_of(nl)
    mine = pl.ds(pl.multiple_of(me * 128, 128), 128)
    stay = [
        pltpu.make_async_copy(w, w_all.at[l], local.at[0]),
        pltpu.make_async_copy(rows.at[me], got.at[me], local.at[1]),
        pltpu.make_async_copy(ups.at[me], got_up.at[me], local.at[2]),
        pltpu.make_async_copy(downs.at[me], got_down.at[:, mine], local.at[3]),
    ]
    shards = [
        remote(w, w_all.at[l], w_send.at[j], w_recv.at[j], (o, lax.rem(l + 2 * j, nl)))
        for j in range(1, half)
    ]
    forwards = [remote(w, w_all.at[l], f_send.at[0], f_recv.at[0], partner)]
    for c in shards:
        c.start()
    start, wait = all_to_all(
        me, nl, n,
        [
            (lambda to: rows.at[to], got.at[me]),
            (lambda to: ups.at[to], got_up.at[me]),
            (lambda to: downs.at[to], got_down.at[:, mine]),
        ],
        a_send, a_recv,
    )
    start()
    forwards[0].start()
    for c in stay:
        c.start()
    for j in range(1, half):
        shards[j - 1].wait_recv()
        block = w_all.at[lax.rem(l - 2 * j + nl, nl)]
        forwards.append(remote(block, block, f_send.at[j], f_recv.at[j], partner))
        forwards[-1].start()
    wait()
    for c in shards:
        c.wait_send()
    for c in forwards:
        c.wait()
    for c in stay:
        c.wait()


def gather_kernel(
    no, nl, down, up, back, all_down, all_up, got,
    a_send, a_recv, z_send, z_recv, x_send, x_recv, f_send, f_recv, local,
):
    n, half = no * nl, nl // 2
    o, l, me, partner = position_of(nl)
    pieces = ((down, all_down), (up, all_up))
    stay = [
        pltpu.make_async_copy(down, all_down.at[me], local.at[0]),
        pltpu.make_async_copy(up, all_up.at[me], local.at[1]),
        pltpu.make_async_copy(back.at[me], got.at[me], local.at[2]),
    ]
    columns, planes, forwards = {}, {}, []
    for k in range(1, no):
        columns[k] = [
            remote(a, b.at[me], z_send.at[i * no + k], z_recv.at[i * no + k], (lax.rem(o + k, no), l))
            for i, (a, b) in enumerate(pieces)
        ]
        for c in columns[k]:
            c.start()
    start, wait = all_to_all(
        me, nl, n, [(lambda to: back.at[to], got.at[me])], a_send, a_recv
    )
    start()

    def forward(k, j, parts):
        block = lax.rem(o - k + no, no) * nl + lax.rem(l - 2 * j + nl, nl)
        for i, (a, b) in enumerate(parts):
            s = (i * no + k) * half + j
            src = b.at[block] if a is None else a
            forwards.append(remote(src, b.at[block], f_send.at[s], f_recv.at[s], partner))
            forwards[-1].start()

    for k in range(no):
        if k > 0:
            for c in columns[k]:
                c.wait_recv()
        block = lax.rem(o - k + no, no) * nl + l
        for j in range(1, half):
            planes[k, j] = []
            for i, (a, b) in enumerate(pieces):
                s = (i * no + k) * half + j
                src = a if k == 0 else b.at[block]
                c = remote(src, b.at[block], x_send.at[s], x_recv.at[s], (o, lax.rem(l + 2 * j, nl)))
                c.start()
                planes[k, j].append(c)
        forward(k, 0, [(a if k == 0 else None, b) for a, b in pieces])
    for c in stay:
        c.start()
    for k in range(no):
        for j in range(1, half):
            for c in planes[k, j]:
                c.wait_recv()
            forward(k, j, [(None, b) for _, b in pieces])
    wait()
    for group in list(columns.values()) + list(planes.values()):
        for c in group:
            c.wait_send()
    for c in forwards:
        c.wait()
    for c in stay:
        c.wait()


def dma(count):
    return pltpu.SemaphoreType.DMA((count,))


def on_device(
    no, nl, tokens, value_base_weight, adapter_down, adapter_up, adapter_per_row, frequent_adapter
):
    n, half = no * nl, nl // 2
    bf16, f32 = jnp.bfloat16, jnp.float32
    width = tokens.shape[1]
    output_width = adapter_up.shape[1]
    me = lax.axis_index(("owner", "lane"))
    part = width // n
    pair = part // 2
    up_rows = max(1, ADAPTER_RANK // n)
    up_parts = ADAPTER_RANK // up_rows

    match = adapter_per_row[:, None] == frequent_adapter[None, :]
    is_hot = jnp.any(match, axis=1)
    owner_dev = adapter_per_row // ADAPTERS_DEVICE
    slot = adapter_per_row % ADAPTERS_DEVICE
    hits = (
        (owner_dev[:, None] == jnp.arange(n, dtype=jnp.int32)[None, :]) & (~is_hot)[:, None]
    ).astype(jnp.int32)
    ranks = jnp.sum(jnp.cumsum(hits, axis=0) * hits, axis=1) - 1
    position = jnp.where(is_hot, n * CAP, owner_dev * CAP + ranks)
    here = position[:, None] == jnp.arange(n * CAP, dtype=jnp.int32)[None, :]
    place = here.astype(bf16)
    send_rows = (
        lax.dot_general(place, tokens, (((0,), (0,)), ((), ())), preferred_element_type=f32)
        .astype(bf16)
        .reshape(n, CAP, width)
    )
    send_slots = jnp.max(jnp.where(here, slot[:, None], -1), axis=0).astype(bf16)

    hot_root = frequent_adapter // ADAPTERS_DEVICE
    hot_slot = frequent_adapter % ADAPTERS_DEVICE
    own_slot = jnp.sum(jnp.where(hot_root == me, hot_slot, 0))
    columns = lax.dynamic_slice_in_dim(adapter_down, own_slot // 2 * 128, 128, 1)
    lanes = jnp.arange(128, dtype=jnp.int32)
    pick = (
        lanes[:, None] == own_slot % 2 * ADAPTER_RANK + lanes[None, :] % ADAPTER_RANK
    ).astype(bf16)
    twice = jnp.dot(columns, pick, preferred_element_type=f32).astype(bf16).reshape(n, 2, pair, 128)
    send_down = jnp.where(lanes < ADAPTER_RANK, twice[:, 0], twice[:, 1])
    own_up = lax.dynamic_slice_in_dim(adapter_up, own_slot * ADAPTER_RANK, ADAPTER_RANK, 0)
    own_up = own_up.reshape(up_parts, up_rows, output_width)
    own_up = jnp.concatenate([own_up] * (n // up_parts), axis=0)
    tags = jnp.broadcast_to(
        send_slots.reshape(n, 1, CAP, 1), (n, up_rows, CAP, output_width // CAP)
    ).reshape(n, up_rows, output_width)
    send_up = jnp.concatenate([own_up, tags], axis=1)

    def shape(*dims):
        return jax.ShapeDtypeStruct(dims, bf16)

    base_weight, arrived, arrived_up, arrived_down = pl.pallas_call(
        functools.partial(exchange_kernel, no, nl),
        out_shape=(
            shape(nl, *value_base_weight.shape),
            shape(n, CAP, width),
            shape(n, 2 * up_rows, output_width),
            shape(pair, n * 128),
        ),
        in_specs=[ANY] * 4,
        out_specs=[ANY] * 4,
        scratch_shapes=[dma(3 * n), dma(3 * n), dma(half), dma(half), dma(half), dma(half), dma(4)],
        compiler_params=pltpu.CompilerParams(has_side_effects=True),
    )(value_base_weight, send_rows, send_up, send_down)

    order = jnp.arange(ADAPTER_RANK * HOT, dtype=jnp.int32)
    hot_of = order // up_rows % HOT
    rank_of = order // (up_rows * HOT) * up_rows + order % up_rows
    source = hot_root[hot_of] * 128 + rank_of
    index = jnp.arange(n * 128, dtype=jnp.int32)[:, None]
    halves = [
        jnp.dot(
            arrived_down,
            (index == (source + h * ADAPTER_RANK)[None, :]).astype(bf16),
            preferred_element_type=f32,
        ).astype(bf16)
        for h in range(2)
    ]
    piece_down = jnp.concatenate(halves, axis=0)
    piece_up = arrived_up[hot_root, :up_rows].reshape(HOT * up_rows, output_width)

    labels = arrived_up[:, up_rows].reshape(n, CAP, output_width // CAP)[:, :, 0]
    labels = labels.reshape(-1).astype(jnp.int32)
    column_holder = jnp.arange(adapter_down.shape[1], dtype=jnp.int32) // ADAPTER_RANK
    rank_projection = jnp.where(
        column_holder[None, :] == labels[:, None],
        jnp.dot(arrived.reshape(-1, width), adapter_down, preferred_element_type=f32),
        0.0,
    ).astype(bf16)
    final_output = jnp.dot(rank_projection, adapter_up, preferred_element_type=f32).astype(bf16)

    hot_down, hot_up, returned = pl.pallas_call(
        functools.partial(gather_kernel, no, nl),
        out_shape=(
            shape(n, *piece_down.shape),
            shape(n, *piece_up.shape),
            shape(n, CAP, output_width),
        ),
        in_specs=[ANY] * 3,
        out_specs=[ANY] * 3,
        scratch_shapes=[
            dma(n), dma(n), dma(2 * no), dma(2 * no),
            dma(2 * no * half), dma(2 * no * half), dma(2 * no * half), dma(2 * no * half), dma(3),
        ],
        compiler_params=pltpu.CompilerParams(has_side_effects=True),
    )(piece_down, piece_up, final_output.reshape(n, CAP, output_width))

    hot_down = hot_down.reshape(width, HOT * ADAPTER_RANK)
    hot_up = hot_up[:up_parts].reshape(HOT * ADAPTER_RANK, output_width)
    hot_shrink = jnp.where(
        adapter_per_row[:, None] == frequent_adapter[hot_of][None, :],
        jnp.dot(tokens, hot_down, preferred_element_type=f32),
        0.0,
    ).astype(bf16)
    adapter_delta = (
        jnp.dot(hot_shrink, hot_up, preferred_element_type=f32)
        + jnp.dot(place, returned.reshape(n * CAP, output_width), preferred_element_type=f32)
    ).astype(bf16)
    base_output = jnp.dot(
        tokens, base_weight.reshape(width, output_width), preferred_element_type=f32
    )
    return (base_output + ADAPTER_SCALE * adapter_delta.astype(f32)).astype(bf16)


def solution(mesh):
    placed = (
        P(("owner", "lane"), None),
        P("lane", None),
        P(None, ("owner", "lane")),
        P(("owner", "lane"), None),
        P(("owner", "lane")),
        P(),
    )
    return jax.shard_map(
        functools.partial(on_device, mesh.shape["owner"], mesh.shape["lane"]),
        mesh=mesh, in_specs=placed, out_specs=P(("owner", "lane"), None), check_vma=False,
    )
```

```python
import functools

import jax
import jax.numpy as jnp
from jax import lax
from jax.experimental import pallas as pl
from jax.experimental.pallas import tpu as pltpu
from jax.sharding import PartitionSpec as P

ADAPTER_RANK = 64
ADAPTERS_DEVICE = 16
HOT = 8
CAP = 4


ADAPTER_SCALE = 2.0


MESH = pl.DeviceIdType.MESH
ANY = pl.BlockSpec(memory_space=pl.ANY)


def remote(src, dst, send, recv, at):
    return pltpu.make_async_remote_copy(
        src_ref=src, dst_ref=dst, send_sem=send, recv_sem=recv, device_id=at, device_id_type=MESH
    )


def position_of(nl):
    o, l = lax.axis_index("owner"), lax.axis_index("lane")
    return o, l, o * nl + l, (o, l + 1 - 2 * lax.rem(l, 2))


def all_to_all(me, nl, n, pairs, send, recv):
    def copies(k):
        to = lax.rem(me + k, n)
        at = (lax.div(to, nl), lax.rem(to, nl))
        return [
            remote(src(to), dst, send.at[i * n + k], recv.at[i * n + k], at)
            for i, (src, dst) in enumerate(pairs)
        ]

    def start():
        @pl.loop(1, n)
        def _(k):
            for c in copies(k):
                c.start()

    def wait():
        @pl.loop(1, n)
        def _(k):
            for c in copies(k):
                c.wait()

    return start, wait


def exchange_kernel(
    no, nl, rows, ups, downs, got, got_up, got_down, a_send, a_recv, local
):
    n = no * nl
    me = position_of(nl)[2]
    stay = [
        pltpu.make_async_copy(rows.at[me], got.at[me], local.at[1]),
        pltpu.make_async_copy(ups.at[me], got_up.at[me], local.at[2]),
        pltpu.make_async_copy(downs.at[me], got_down.at[me], local.at[3]),
    ]
    start, wait = all_to_all(
        me, nl, n,
        [
            (lambda to: rows.at[to], got.at[me]),
            (lambda to: ups.at[to], got_up.at[me]),
            (lambda to: downs.at[to], got_down.at[me]),
        ],
        a_send, a_recv,
    )
    start()
    for c in stay:
        c.start()
    wait()
    for c in stay:
        c.wait()


def gather_kernel(no, nl, down, up, back, *refs):
    n, half = no * nl, nl // 2
    shards, refs = refs[:half], refs[half:]
    (all_down, all_up, got, other, a_send, a_recv, z_send, z_recv, x_send, x_recv,
     f_send, f_recv, w_send, w_recv, local) = refs
    o, l, me, partner = position_of(nl)
    pieces = ((down, all_down), (up, all_up))
    stay = [
        pltpu.make_async_copy(down, all_down.at[me], local.at[0]),
        pltpu.make_async_copy(up, all_up.at[me], local.at[1]),
        pltpu.make_async_copy(back.at[me], got.at[me], local.at[2]),
    ]
    columns, planes, forwards = {}, {}, []
    for k in range(1, no):
        columns[k] = [
            remote(a, b.at[me], z_send.at[i * no + k], z_recv.at[i * no + k], (lax.rem(o + k, no), l))
            for i, (a, b) in enumerate(pieces)
        ]
        for c in columns[k]:
            c.start()
    start, wait = all_to_all(
        me, nl, n, [(lambda to: back.at[to], got.at[me])], a_send, a_recv
    )
    start()

    def forward(k, j, parts):
        block = lax.rem(o - k + no, no) * nl + lax.rem(l - 2 * j + nl, nl)
        for i, (a, b) in enumerate(parts):
            s = (i * no + k) * half + j
            src = b.at[block] if a is None else a
            forwards.append(remote(src, b.at[block], f_send.at[s], f_recv.at[s], partner))
            forwards[-1].start()

    for j in range(half):
        c = remote(shards[j], other.at[j], w_send.at[j], w_recv.at[j], partner)
        c.start()
        forwards.append(c)
    for k in range(no):
        if k > 0:
            for c in columns[k]:
                c.wait_recv()
        block = lax.rem(o - k + no, no) * nl + l
        for j in range(1, half):
            planes[k, j] = []
            for i, (a, b) in enumerate(pieces):
                s = (i * no + k) * half + j
                src = a if k == 0 else b.at[block]
                c = remote(src, b.at[block], x_send.at[s], x_recv.at[s], (o, lax.rem(l + 2 * j, nl)))
                c.start()
                planes[k, j].append(c)
        forward(k, 0, [(a if k == 0 else None, b) for a, b in pieces])
    for c in stay:
        c.start()
    for k in range(no):
        for j in range(1, half):
            for c in planes[k, j]:
                c.wait_recv()
            forward(k, j, [(None, b) for _, b in pieces])
    wait()
    for group in list(columns.values()) + list(planes.values()):
        for c in group:
            c.wait_send()
    for c in forwards:
        c.wait()
    for c in stay:
        c.wait()


def finish_kernel(nl, tokens, shrink, place, other, up, returned, *refs):
    half = nl // 2
    shards, out = refs[:half], refs[half]
    l = lax.axis_index("lane")
    depth = shards[0].shape[0]
    f32 = jnp.float32
    delta = jnp.dot(shrink[...], up[...], preferred_element_type=f32)
    delta += jnp.dot(place[...], returned[...], preferred_element_type=f32)
    delta = delta.astype(jnp.bfloat16).astype(f32)
    base = None
    for j in range(half):
        owner = lax.rem(l - 2 * j + nl, nl)
        for lane, block in ((owner, shards[j]), (owner + 1 - 2 * lax.rem(owner, 2), other.at[j])):
            columns = pl.ds(pl.multiple_of(lane * depth, depth), depth)
            term = jnp.dot(tokens[:, columns], block[...], preferred_element_type=f32)
            base = term if base is None else base + term
    out[...] = (base + ADAPTER_SCALE * delta).astype(out.dtype)


def dma(count):
    return pltpu.SemaphoreType.DMA((count,))


def on_device(
    no, nl, tokens, value_base_weight, adapter_down, adapter_up, adapter_per_row, frequent_adapter
):
    n, half = no * nl, nl // 2
    bf16, f32 = jnp.bfloat16, jnp.float32
    width = tokens.shape[1]
    output_width = adapter_up.shape[1]
    me = lax.axis_index(("owner", "lane"))
    part = width // n
    pair = part // 2
    up_rows = max(1, ADAPTER_RANK // n)
    up_parts = ADAPTER_RANK // up_rows

    match = adapter_per_row[:, None] == frequent_adapter[None, :]
    is_hot = jnp.any(match, axis=1)
    owner_dev = adapter_per_row // ADAPTERS_DEVICE
    slot = adapter_per_row % ADAPTERS_DEVICE
    hits = (
        (owner_dev[:, None] == jnp.arange(n, dtype=jnp.int32)[None, :]) & (~is_hot)[:, None]
    ).astype(jnp.int32)
    ranks = jnp.sum(jnp.cumsum(hits, axis=0) * hits, axis=1) - 1
    position = jnp.where(is_hot, n * CAP, owner_dev * CAP + ranks)
    here = position[:, None] == jnp.arange(n * CAP, dtype=jnp.int32)[None, :]
    place = here.astype(bf16)
    send_rows = (
        lax.dot_general(place, tokens, (((0,), (0,)), ((), ())), preferred_element_type=f32)
        .astype(bf16)
        .reshape(n, CAP, width)
    )
    send_slots = jnp.max(jnp.where(here, slot[:, None], -1), axis=0).astype(bf16)

    hot_root = frequent_adapter // ADAPTERS_DEVICE
    hot_slot = frequent_adapter % ADAPTERS_DEVICE
    own_slot = jnp.sum(jnp.where(hot_root == me, hot_slot, 0))
    columns = lax.dynamic_slice_in_dim(adapter_down, own_slot // 2 * 128, 128, 1)
    lanes = jnp.arange(128, dtype=jnp.int32)
    pick = (
        lanes[:, None] == own_slot % 2 * ADAPTER_RANK + lanes[None, :] % ADAPTER_RANK
    ).astype(bf16)
    twice = jnp.dot(columns, pick, preferred_element_type=f32).astype(bf16).reshape(n, 2, pair, 128)
    send_down = jnp.where(lanes < ADAPTER_RANK, twice[:, 0], twice[:, 1])
    own_up = lax.dynamic_slice_in_dim(adapter_up, own_slot * ADAPTER_RANK, ADAPTER_RANK, 0)
    own_up = own_up.reshape(up_parts, up_rows, output_width)
    own_up = jnp.concatenate([own_up] * (n // up_parts), axis=0)
    tags = jnp.broadcast_to(
        send_slots.reshape(n, 1, CAP, 1), (n, up_rows, CAP, output_width // CAP)
    ).reshape(n, up_rows, output_width)
    send_up = jnp.concatenate([own_up, tags], axis=1)

    def shape(*dims):
        return jax.ShapeDtypeStruct(dims, bf16)

    shards = [value_base_weight] + [
        lax.ppermute(value_base_weight, "lane", [(i, (i + 2 * j) % nl) for i in range(nl)])
        for j in range(1, half)
    ]
    arrived, arrived_up, arrived_down = pl.pallas_call(
        functools.partial(exchange_kernel, no, nl),
        out_shape=(
            shape(n, CAP, width),
            shape(n, 2 * up_rows, output_width),
            shape(n, pair, 128),
        ),
        in_specs=[ANY] * 3,
        out_specs=[ANY] * 3,
        scratch_shapes=[dma(3 * n), dma(3 * n), dma(4)],
        compiler_params=pltpu.CompilerParams(has_side_effects=True),
    )(send_rows, send_up, send_down)

    order = jnp.arange(ADAPTER_RANK * HOT, dtype=jnp.int32)
    hot_of = order // up_rows % HOT
    rank_of = order // (up_rows * HOT) * up_rows + order % up_rows
    source = hot_of * 128 + rank_of
    index = jnp.arange(HOT * 128, dtype=jnp.int32)[:, None]
    hot_arrived = arrived_down[hot_root].transpose(1, 0, 2).reshape(pair, HOT * 128)
    halves = [
        jnp.dot(
            hot_arrived,
            (index == (source + h * ADAPTER_RANK)[None, :]).astype(bf16),
            preferred_element_type=f32,
        ).astype(bf16)
        for h in range(2)
    ]
    piece_down = jnp.concatenate(halves, axis=0)
    piece_up = arrived_up[hot_root, :up_rows].reshape(HOT * up_rows, output_width)

    labels = arrived_up[:, up_rows].reshape(n, CAP, output_width // CAP)[:, :, 0]
    labels = labels.reshape(-1).astype(jnp.int32)
    column_holder = jnp.arange(adapter_down.shape[1], dtype=jnp.int32) // ADAPTER_RANK
    rank_projection = jnp.where(
        column_holder[None, :] == labels[:, None],
        jnp.dot(arrived.reshape(-1, width), adapter_down, preferred_element_type=f32),
        0.0,
    ).astype(bf16)
    final_output = jnp.dot(rank_projection, adapter_up, preferred_element_type=f32).astype(bf16)

    hot_down, hot_up, returned, other = pl.pallas_call(
        functools.partial(gather_kernel, no, nl),
        out_shape=(
            shape(n, *piece_down.shape),
            shape(n, *piece_up.shape),
            shape(n, CAP, output_width),
            shape(half, *value_base_weight.shape),
        ),
        in_specs=[ANY] * (3 + half),
        out_specs=[ANY] * 4,
        scratch_shapes=[
            dma(n), dma(n), dma(2 * no), dma(2 * no),
            dma(2 * no * half), dma(2 * no * half), dma(2 * no * half), dma(2 * no * half),
            dma(half), dma(half), dma(3),
        ],
        compiler_params=pltpu.CompilerParams(has_side_effects=True),
    )(piece_down, piece_up, final_output.reshape(n, CAP, output_width), *shards)

    hot_down = hot_down.reshape(width, HOT * ADAPTER_RANK)
    hot_up = hot_up[:up_parts].reshape(HOT * ADAPTER_RANK, output_width)
    hot_shrink = jnp.where(
        adapter_per_row[:, None] == frequent_adapter[hot_of][None, :],
        jnp.dot(tokens, hot_down, preferred_element_type=f32),
        0.0,
    ).astype(bf16)
    rows, depth, tile = tokens.shape[0], value_base_weight.shape[0], 256

    def whole(array):
        return pl.BlockSpec(array.shape, lambda i: (0, 0))

    def strip(height):
        return pl.BlockSpec((height, tile), lambda i: (0, i))

    return pl.pallas_call(
        functools.partial(finish_kernel, nl),
        out_shape=shape(rows, output_width),
        grid=(output_width // tile,),
        in_specs=[
            whole(tokens), whole(hot_shrink), whole(place),
            pl.BlockSpec((half, depth, tile), lambda i: (0, 0, i)),
            strip(hot_up.shape[0]), strip(n * CAP),
        ] + [strip(depth)] * half,
        out_specs=strip(rows),
    )(tokens, hot_shrink, place, other, hot_up, returned.reshape(n * CAP, output_width), *shards)


def solution(mesh):
    placed = (
        P(("owner", "lane"), None),
        P("lane", None),
        P(None, ("owner", "lane")),
        P(("owner", "lane"), None),
        P(("owner", "lane")),
        P(),
    )
    return jax.shard_map(
        functools.partial(on_device, mesh.shape["owner"], mesh.shape["lane"]),
        mesh=mesh, in_specs=placed, out_specs=P(("owner", "lane"), None), check_vma=False,
    )
```

```python
import functools

import jax
import jax.numpy as jnp
from jax import lax
from jax.experimental import pallas as pl
from jax.experimental.pallas import tpu as pltpu
from jax.sharding import PartitionSpec as P

ADAPTER_RANK = 64
ADAPTERS_DEVICE = 16
HOT = 8
CAP = 4


ADAPTER_SCALE = 2.0


MESH = pl.DeviceIdType.MESH
ANY = pl.BlockSpec(memory_space=pl.ANY)


def remote(src, dst, send, recv, at):
    return pltpu.make_async_remote_copy(
        src_ref=src, dst_ref=dst, send_sem=send, recv_sem=recv, device_id=at, device_id_type=MESH
    )


def position_of(nl):
    o, l = lax.axis_index("owner"), lax.axis_index("lane")
    return o, l, o * nl + l, (o, l + 1 - 2 * lax.rem(l, 2))


def all_to_all(me, nl, n, pairs, send, recv):
    def copies(k):
        to = lax.rem(me + k, n)
        at = (lax.div(to, nl), lax.rem(to, nl))
        return [
            remote(src(to), dst, send.at[i * n + k], recv.at[i * n + k], at)
            for i, (src, dst) in enumerate(pairs)
        ]

    def start():
        @pl.loop(1, n)
        def _(k):
            for c in copies(k):
                c.start()

    def wait():
        @pl.loop(1, n)
        def _(k):
            for c in copies(k):
                c.wait()

    return start, wait


def exchange_kernel(
    no, nl, rows, ups, downs, tags, got, got_up, got_down, got_tag, a_send, a_recv, local
):
    n = no * nl
    me = position_of(nl)[2]
    stay = [
        pltpu.make_async_copy(rows.at[me], got.at[me], local.at[1]),
        pltpu.make_async_copy(ups.at[me], got_up.at[me], local.at[2]),
        pltpu.make_async_copy(downs.at[me], got_down.at[me], local.at[3]),
        pltpu.make_async_copy(tags.at[me], got_tag.at[me], local.at[0]),
    ]
    start, wait = all_to_all(
        me, nl, n,
        [
            (lambda to: rows.at[to], got.at[me]),
            (lambda to: ups.at[to], got_up.at[me]),
            (lambda to: downs.at[to], got_down.at[me]),
            (lambda to: tags.at[to], got_tag.at[me]),
        ],
        a_send, a_recv,
    )
    start()
    for c in stay:
        c.start()
    wait()
    for c in stay:
        c.wait()


def gather_kernel(no, nl, down, up, back, *refs):
    n, half = no * nl, nl // 2
    shards, refs = refs[:half], refs[half:]
    (all_down, all_up, got, other, a_send, a_recv, z_send, z_recv, x_send, x_recv,
     f_send, f_recv, w_send, w_recv, local) = refs
    o, l, me, partner = position_of(nl)
    pieces = ((down, all_down), (up, all_up))
    stay = [
        pltpu.make_async_copy(down, all_down.at[me], local.at[0]),
        pltpu.make_async_copy(up, all_up.at[me], local.at[1]),
        pltpu.make_async_copy(back.at[me], got.at[me], local.at[2]),
    ]
    columns, planes, forwards = {}, {}, []
    for k in range(1, no):
        columns[k] = [
            remote(a, b.at[me], z_send.at[i * no + k], z_recv.at[i * no + k], (lax.rem(o + k, no), l))
            for i, (a, b) in enumerate(pieces)
        ]
        for c in columns[k]:
            c.start()
    start, wait = all_to_all(
        me, nl, n, [(lambda to: back.at[to], got.at[me])], a_send, a_recv
    )
    start()

    def forward(k, j, parts):
        block = lax.rem(o - k + no, no) * nl + lax.rem(l - 2 * j + nl, nl)
        for i, (a, b) in enumerate(parts):
            s = (i * no + k) * half + j
            src = b.at[block] if a is None else a
            forwards.append(remote(src, b.at[block], f_send.at[s], f_recv.at[s], partner))
            forwards[-1].start()

    for j in range(half):
        c = remote(shards[j], other.at[j], w_send.at[j], w_recv.at[j], partner)
        c.start()
        forwards.append(c)
    for k in range(no):
        if k > 0:
            for c in columns[k]:
                c.wait_recv()
        block = lax.rem(o - k + no, no) * nl + l
        for j in range(1, half):
            planes[k, j] = []
            for i, (a, b) in enumerate(pieces):
                s = (i * no + k) * half + j
                src = a if k == 0 else b.at[block]
                c = remote(src, b.at[block], x_send.at[s], x_recv.at[s], (o, lax.rem(l + 2 * j, nl)))
                c.start()
                planes[k, j].append(c)
        forward(k, 0, [(a if k == 0 else None, b) for a, b in pieces])
    for c in stay:
        c.start()
    for k in range(no):
        for j in range(1, half):
            for c in planes[k, j]:
                c.wait_recv()
            forward(k, j, [(None, b) for _, b in pieces])
    wait()
    for group in list(columns.values()) + list(planes.values()):
        for c in group:
            c.wait_send()
    for c in forwards:
        c.wait()
    for c in stay:
        c.wait()


def finish_kernel(nl, tokens, shrink, place, other, up, returned, *refs):
    half = nl // 2
    shards, out = refs[:half], refs[half]
    l = lax.axis_index("lane")
    depth = shards[0].shape[0]
    f32 = jnp.float32
    delta = jnp.dot(shrink[...], up[...], preferred_element_type=f32)
    delta += jnp.dot(place[...], returned[...], preferred_element_type=f32)
    delta = delta.astype(jnp.bfloat16).astype(f32)
    base = None
    for j in range(half):
        owner = lax.rem(l - 2 * j + nl, nl)
        for lane, block in ((owner, shards[j]), (owner + 1 - 2 * lax.rem(owner, 2), other.at[j])):
            columns = pl.ds(pl.multiple_of(lane * depth, depth), depth)
            term = jnp.dot(tokens[:, columns], block[...], preferred_element_type=f32)
            base = term if base is None else base + term
    out[...] = (base + ADAPTER_SCALE * delta).astype(out.dtype)


def dma(count):
    return pltpu.SemaphoreType.DMA((count,))


def on_device(
    no, nl, tokens, value_base_weight, adapter_down, adapter_up, adapter_per_row, frequent_adapter
):
    n, half = no * nl, nl // 2
    bf16, f32 = jnp.bfloat16, jnp.float32
    width = tokens.shape[1]
    output_width = adapter_up.shape[1]
    me = lax.axis_index(("owner", "lane"))
    part = width // n
    pair = part // 2
    up_rows = max(1, ADAPTER_RANK // n)
    up_parts = ADAPTER_RANK // up_rows

    match = adapter_per_row[:, None] == frequent_adapter[None, :]
    is_hot = jnp.any(match, axis=1)
    owner_dev = adapter_per_row // ADAPTERS_DEVICE
    slot = adapter_per_row % ADAPTERS_DEVICE
    hits = (
        (owner_dev[:, None] == jnp.arange(n, dtype=jnp.int32)[None, :]) & (~is_hot)[:, None]
    ).astype(jnp.int32)
    ranks = jnp.sum(jnp.cumsum(hits, axis=0) * hits, axis=1) - 1
    position = jnp.where(is_hot, n * CAP, owner_dev * CAP + ranks)
    here = position[:, None] == jnp.arange(n * CAP, dtype=jnp.int32)[None, :]
    place = here.astype(bf16)
    send_rows = (
        lax.dot_general(place, tokens, (((0,), (0,)), ((), ())), preferred_element_type=f32)
        .astype(bf16)
        .reshape(n, CAP, width)
    )
    send_slots = jnp.max(jnp.where(here, slot[:, None], -1), axis=0).astype(bf16)

    hot_root = frequent_adapter // ADAPTERS_DEVICE
    hot_slot = frequent_adapter % ADAPTERS_DEVICE
    own_slot = jnp.sum(jnp.where(hot_root == me, hot_slot, 0))
    columns = lax.dynamic_slice_in_dim(adapter_down, own_slot // 2 * 128, 128, 1)
    lanes = jnp.arange(128, dtype=jnp.int32)
    pick = (
        lanes[:, None] == own_slot % 2 * ADAPTER_RANK + lanes[None, :] % ADAPTER_RANK
    ).astype(bf16)
    twice = jnp.dot(columns, pick, preferred_element_type=f32).astype(bf16).reshape(n, 2, pair, 128)
    send_down = jnp.where(lanes < ADAPTER_RANK, twice[:, 0], twice[:, 1])
    own_up = lax.dynamic_slice_in_dim(adapter_up, own_slot * ADAPTER_RANK, ADAPTER_RANK, 0)
    own_up = own_up.reshape(up_parts, up_rows, output_width)
    send_up = jnp.concatenate([own_up] * (n // up_parts), axis=0)
    send_tags = jnp.broadcast_to(send_slots.reshape(n, CAP, 1), (n, CAP, 128))

    def shape(*dims):
        return jax.ShapeDtypeStruct(dims, bf16)

    shards = [value_base_weight] + [
        lax.ppermute(value_base_weight, "lane", [(i, (i + 2 * j) % nl) for i in range(nl)])
        for j in range(1, half)
    ]
    arrived, arrived_up, arrived_down, arrived_tags = pl.pallas_call(
        functools.partial(exchange_kernel, no, nl),
        out_shape=(
            shape(n, CAP, width),
            shape(n, up_rows, output_width),
            shape(n, pair, 128),
            shape(n, CAP, 128),
        ),
        in_specs=[ANY] * 4,
        out_specs=[ANY] * 4,
        scratch_shapes=[dma(4 * n), dma(4 * n), dma(4)],
        compiler_params=pltpu.CompilerParams(has_side_effects=True),
    )(send_rows, send_up, send_down, send_tags)

    order = jnp.arange(ADAPTER_RANK * HOT, dtype=jnp.int32)
    hot_of = order // up_rows % HOT
    rank_of = order // (up_rows * HOT) * up_rows + order % up_rows
    source = hot_of * 128 + rank_of
    index = jnp.arange(HOT * 128, dtype=jnp.int32)[:, None]
    hot_arrived = arrived_down[hot_root].transpose(1, 0, 2).reshape(pair, HOT * 128)
    halves = [
        jnp.dot(
            hot_arrived,
            (index == (source + h * ADAPTER_RANK)[None, :]).astype(bf16),
            preferred_element_type=f32,
        ).astype(bf16)
        for h in range(2)
    ]
    piece_down = jnp.concatenate(halves, axis=0)
    piece_up = arrived_up[hot_root].reshape(HOT * up_rows, output_width)

    labels = arrived_tags[:, :, 0].reshape(-1).astype(jnp.int32)
    column_holder = jnp.arange(adapter_down.shape[1], dtype=jnp.int32) // ADAPTER_RANK
    rank_projection = jnp.where(
        column_holder[None, :] == labels[:, None],
        jnp.dot(arrived.reshape(-1, width), adapter_down, preferred_element_type=f32),
        0.0,
    ).astype(bf16)
    final_output = jnp.dot(rank_projection, adapter_up, preferred_element_type=f32).astype(bf16)

    hot_down, hot_up, returned, other = pl.pallas_call(
        functools.partial(gather_kernel, no, nl),
        out_shape=(
            shape(n, *piece_down.shape),
            shape(n, *piece_up.shape),
            shape(n, CAP, output_width),
            shape(half, *value_base_weight.shape),
        ),
        in_specs=[ANY] * (3 + half),
        out_specs=[ANY] * 4,
        scratch_shapes=[
            dma(n), dma(n), dma(2 * no), dma(2 * no),
            dma(2 * no * half), dma(2 * no * half), dma(2 * no * half), dma(2 * no * half),
            dma(half), dma(half), dma(3),
        ],
        compiler_params=pltpu.CompilerParams(has_side_effects=True),
    )(piece_down, piece_up, final_output.reshape(n, CAP, output_width), *shards)

    hot_down = hot_down.reshape(width, HOT * ADAPTER_RANK)
    hot_up = hot_up[:up_parts].reshape(HOT * ADAPTER_RANK, output_width)
    hot_here = jnp.sum(
        jnp.where(
            hot_of[:, None] == jnp.arange(HOT, dtype=jnp.int32)[None, :], frequent_adapter[None, :], 0
        ),
        axis=1,
    )
    hot_shrink = jnp.where(
        adapter_per_row[:, None] == hot_here[None, :],
        jnp.dot(tokens, hot_down, preferred_element_type=f32),
        0.0,
    ).astype(bf16)
    rows, depth, tile = tokens.shape[0], value_base_weight.shape[0], 256

    def whole(array):
        return pl.BlockSpec(array.shape, lambda i: (0, 0))

    def strip(height):
        return pl.BlockSpec((height, tile), lambda i: (0, i))

    return pl.pallas_call(
        functools.partial(finish_kernel, nl),
        out_shape=shape(rows, output_width),
        grid=(output_width // tile,),
        in_specs=[
            whole(tokens), whole(hot_shrink), whole(place),
            pl.BlockSpec((half, depth, tile), lambda i: (0, 0, i)),
            strip(hot_up.shape[0]), strip(n * CAP),
        ] + [strip(depth)] * half,
        out_specs=strip(rows),
    )(tokens, hot_shrink, place, other, hot_up, returned.reshape(n * CAP, output_width), *shards)


def solution(mesh):
    placed = (
        P(("owner", "lane"), None),
        P("lane", None),
        P(None, ("owner", "lane")),
        P(("owner", "lane"), None),
        P(("owner", "lane")),
        P(),
    )
    return jax.shard_map(
        functools.partial(on_device, mesh.shape["owner"], mesh.shape["lane"]),
        mesh=mesh, in_specs=placed, out_specs=P(("owner", "lane"), None), check_vma=False,
    )
```
